256 devices in a mesh: pair: 4 (over y), ep: 64 (over x, z, core).
Axes of the slice: x: 4, y: 4, z: 8, core: 2. Of those that a mesh axis runs over, the one named last changes fastest.
Arguments:
- hidden: float32 [4, 2048, 2048], P('pair', 'ep'), may hold values from -6 to 6
- moe_gain: float32 [2048], replicated, may hold values from 0.25 to 1.75
- expert_ids: int32 [4, 2048, 2], P('pair', 'ep'), may hold values from 0 to 31, all different within a row; in each aligned block of 32 rows (0 to 31, 32 to 63, ..., all dimensions but the last counted through in order) at most 4 rows name the same one
- gate_weights: float32 [4, 2048, 2], P('pair', 'ep'), may hold values from 0.2 to 1
- w_gate: bfloat16 [64, 2048, 2048], P('ep', None, 'pair'), may hold values from -0.125 to 0.125
- w_up: bfloat16 [64, 2048, 2048], P('ep', None, 'pair'), may hold values from -0.125 to 0.125
- w_down: bfloat16 [64, 2048, 2048], P('ep', 'pair'), may hold values from -0.09375 to 0.09375
- final_gain: float32 [2048], replicated, may hold values from 0.25 to 1.75
- w_out: bfloat16 [2048, 128], replicated, may hold values from -0.125 to 0.125
- latent: float32 [4, 2048, 64], P('pair', 'ep'), may hold values from -6 to 6
- w_in: bfloat16 [128, 2048], replicated, may hold values from -0.5 to 0.5
- modulation: float32 [4, 2, 2048], P('pair'), may hold values from -3 to 16, as said below
- w_qkv: bfloat16 [2048, 3072], P(None, 'pair'), may hold values from -0.125 to 0.125
Outputs:
- latent_next: float32 [4, 2048, 64], P('pair', 'ep')
- attended: bfloat16 [4, 2048, 1024], P('pair', 'ep')
The draws below stay inside these ranges and needn't reach their ends.
Inputs may be any that keep to these rules, and one draw needn't show every extreme that they name: `expert_ids`: within the 32 frames of each device no expert is named more than 4 times, a bound that some block reaches; the two experts of a frame differ. `modulation`: row 0 is a shift, row 1 a positive scale.
All inputs are finite; a program needn't handle non-finite values.
Results may differ from the reference program's by a relative error of at most 0.03.
Values may be sent and summed in bfloat16 or wider, within the bound.
No kernel may reach another device: no remote copies, remote signals or barrier semaphores. Data moves between devices by JAX's collectives and lax.ppermute only.
A program may use at most 64 MiB of HBM per device.

```python
import math
import jax
import jax.numpy as jnp
import numpy as np
from jax import lax

D = 2048
HID = 4096
HEADS = 8
HDIM = 128
CH = 64
TOK_DEV = 32
EXPERTS = 32
CAP = 4
GROUPS = 4
FRAMES = 2048
C = 128
HD = 1024
N_PAIR = 4
N_EP = 64


def draw_modulation(key, part):
    shift_key, scale_key = jax.random.split(jax.random.fold_in(key, 17))
    shift_row = jnp.clip(0.5 * jax.random.normal(shift_key, (GROUPS, 1, D), jnp.float32), -3.0, 3.0)
    scale_row = jnp.exp(jax.random.uniform(scale_key, (GROUPS, 1, D), jnp.float32, math.log(0.5), math.log(2.0)))
    return jnp.concatenate([shift_row, scale_row], 1)


def level_of(rng, extent, shards, least, top_value):
    def one(position, shards_of):
        steps = jax.random.uniform(jax.random.fold_in(jax.random.fold_in(rng, 6), position), (shards_of,), jnp.float32, least / len(shards), top_value / len(shards))
        return jnp.repeat(jnp.exp(steps), extent[position] // shards_of).reshape((-1,) + (1,) * (len(extent) - position - 1))

    loudness = one(*shards[0])
    for cut in shards[1:]:
        loudness = loudness * one(*cut)
    return loudness


def assign_block(rng, own, number, rows, number_of, top, most, lean):
    ranking = jax.random.permutation(rng, number_of)
    heavy_load, usual = load_shares(number_of, rows * top, most, lean, True), load_shares(number_of, rows * top, most, lean, False)
    places = jnp.arange(number_of)

    def named(tallies, rotation):
        used = int((tallies > 0).sum())
        fixed = max(1, used // 4)
        shifted = fixed + (places - fixed + rotation * (used - fixed)) % max(1, number_of - fixed)
        return jnp.zeros((number_of,), jnp.int32).at[ranking[jnp.where(places < fixed, places, shifted)]].set(jnp.asarray(tallies, jnp.int32))

    tallies = jnp.where(number % 4 == 0, named(heavy_load, number // 4), named(usual, number - number // 4 - 1))
    mixed = jax.random.permutation(jax.random.fold_in(own, 3), number_of)
    giver, receiver = mixed[0:number_of // 2 * 2:2], mixed[1:number_of // 2 * 2:2]
    room = jnp.minimum(tallies[giver] - 1, most - tallies[receiver]) // 2
    room = jnp.where((giver == ranking[0]) | (receiver == ranking[0]) | (tallies[receiver] == 0), 0, jnp.maximum(room, 0))
    shifted = jax.random.randint(jax.random.fold_in(own, 4), (number_of // 2,), 0, 1 << 20) % (room + 1)
    tallies = tallies.at[giver].add(-shifted).at[receiver].add(shifted)
    labels = jnp.searchsorted(jnp.cumsum(tallies), jnp.arange(rows * top), side="right").astype(jnp.int32)
    table = labels.reshape(top, rows).T
    table = table[jax.random.permutation(jax.random.fold_in(own, 1), rows)]
    rotation = jax.random.randint(jax.random.fold_in(own, 2), (rows, 1), 0, top)
    return jnp.take_along_axis(table, (jnp.arange(top)[None, :] + rotation) % top, axis=1)


def load_shares(number_of, total, reach, skew, full):
    weights = [(1 << 20) // math.isqrt(rank ** skew) + 1 for rank in range(1, number_of + 1)]
    largest = reach if full else min(reach, max(-(-total // number_of), total * weights[0] // sum(weights)))
    least = 1 if total - largest >= number_of - 1 else 0
    holding, spare = [largest] + [least] * (number_of - 1), total - largest - least * (number_of - 1)
    while spare > 0:
        movable = [i for i in range(1, number_of) if holding[i] < largest] or [i for i in range(1, number_of) if holding[i] < reach]
        mass, left = sum([weights[i] for i in movable]), spare
        for i in movable:
            extra = min(reach - holding[i], max(1, left * weights[i] // mass), spare)
            holding[i] = holding[i] + extra
            spare = spare - extra
    return np.array(holding)


def scatter_about(own_key, extent, width, bound, shards=(), held_as=jnp.bfloat16):
    entries = width * jax.random.normal(own_key, extent, jnp.float32)
    if shards:
        entries = entries * level_of(own_key, extent, shards, -0.22, 0.18)
    return jnp.clip(entries, -bound, bound).astype(held_as)


def setup_inputs(seed: int = 0) -> dict:
    arg_keys = jax.random.split(jax.random.key(seed), 14)
    hidden = scatter_about(arg_keys[0], (GROUPS, FRAMES, D), 1.0, 6.0, ((0, 4), (1, 64)), jnp.float32)
    moe_gain = jnp.clip(1.0 + 0.15 * jax.random.normal(arg_keys[1], (D,), jnp.float32), 0.25, 1.75)
    expert_ids_keys = jax.random.split(jax.random.fold_in(arg_keys[2], 1), GROUPS * FRAMES // TOK_DEV)
    expert_ids_turns = jax.random.permutation(jax.random.fold_in(arg_keys[2], 3), GROUPS * FRAMES // TOK_DEV)
    expert_ids = jax.vmap(lambda own, number: assign_block(jax.random.fold_in(arg_keys[2], 2), own, number, TOK_DEV, EXPERTS, 2, CAP, 2))(expert_ids_keys, expert_ids_turns).reshape((GROUPS, FRAMES, 2))
    gate_weights = jnp.clip(0.2 + 0.8 * jax.random.uniform(arg_keys[3], (GROUPS, FRAMES, 2), jnp.float32) ** level_of(arg_keys[3], (GROUPS, FRAMES, 2), ((0, 4), (1, 64)), -0.2, 0.2), 0.2, 1.0)
    w_gate = scatter_about(arg_keys[4], (2 * EXPERTS, D, HID // 2), D ** -0.5, 0.125, ((0, 64), (2, 4)))
    w_up = scatter_about(arg_keys[5], (2 * EXPERTS, D, HID // 2), D ** -0.5, 0.125, ((0, 64), (2, 4)))
    w_down = scatter_about(arg_keys[6], (2 * EXPERTS, HID // 2, D), HID ** -0.5, 0.09375, ((0, 64), (1, 4)))
    final_gain = jnp.clip(1.0 + 0.15 * jax.random.normal(arg_keys[7], (D,), jnp.float32), 0.25, 1.75)
    w_out = scatter_about(arg_keys[8], (D, C), D ** -0.5, 0.125)
    latent = scatter_about(arg_keys[9], (GROUPS, FRAMES, CH), 1.0, 6.0, ((0, 4), (1, 64)), jnp.float32)
    w_in = scatter_about(arg_keys[10], (C, D), C ** -0.5, 0.5)
    modulation = draw_modulation(jax.random.fold_in(arg_keys[13], 71), 0)
    w_qkv = scatter_about(arg_keys[12], (D, 3 * HD), D ** -0.5, 0.125, ((1, 4),))
    return dict(hidden=hidden, moe_gain=moe_gain, expert_ids=expert_ids, gate_weights=gate_weights, w_gate=w_gate, w_up=w_up, w_down=w_down, final_gain=final_gain, w_out=w_out, latent=latent, w_in=w_in, modulation=modulation, w_qkv=w_qkv)


EPSILON = 1e-06
GUIDANCE = 3.0
STEP_SIZE = 0.25

def rms_scale(values):
    return values * lax.rsqrt(lax.optimization_barrier(jnp.mean(values * values, -1, keepdims=True)) + EPSILON)

def expert_half(block_rows, gate_mat, up_mat, down_mat):
    quarter = gate_mat.shape[1] // N_PAIR
    gated = jnp.dot(block_rows, gate_mat, preferred_element_type=jnp.float32)
    upward = jnp.dot(block_rows, up_mat, preferred_element_type=jnp.float32)
    active = (jax.nn.silu(gated) * upward).astype(jnp.bfloat16)
    partial_sums = jnp.einsum('rqs,qsd->qrd', active.reshape(block_rows.shape[0], N_PAIR, quarter).astype(jnp.float32), down_mat.reshape(N_PAIR, quarter, D).astype(jnp.float32), precision=lax.Precision.HIGHEST)
    rounded = lax.optimization_barrier(partial_sums.astype(jnp.bfloat16))
    return lax.optimization_barrier(jnp.sum(rounded.astype(jnp.float32), 0)).astype(jnp.bfloat16)

def group_velocity(hidden_row, ids_row, gates_row, moe_gain, w_gate, w_up, w_down, final_gain, w_out):
    experts = N_EP // 2
    capacity = 4 * TOK_DEV // experts
    slot_total = N_EP * capacity
    normed = (rms_scale(hidden_row) * moe_gain).astype(jnp.bfloat16)
    flat_ids = ids_row.reshape(N_EP, TOK_DEV * 2).astype(jnp.int32)
    onehot = (flat_ids[:, :, None] == jnp.arange(experts, dtype=jnp.int32)[None, None, :]).astype(jnp.int32)
    slot_rank = lax.optimization_barrier(jnp.sum((jnp.cumsum(onehot, 1) - onehot) * onehot, -1)).astype(jnp.int32)
    sources = jnp.arange(N_EP, dtype=jnp.int32)[:, None]
    places = (flat_ids * slot_total + sources * capacity + slot_rank).reshape(-1).astype(jnp.int32)
    frame_ids = jnp.repeat(jnp.arange(FRAMES, dtype=jnp.int32), 2)
    table = jnp.full((experts * slot_total,), FRAMES, jnp.int32).at[places].set(frame_ids)
    padded = jnp.concatenate([normed, jnp.zeros((1, D), jnp.bfloat16)], 0)

    def run_expert(expert):
        picks = lax.dynamic_slice_in_dim(table, expert * slot_total, slot_total)
        block_rows = padded[picks]
        first_half = expert_half(block_rows, w_gate[2 * expert], w_up[2 * expert], w_down[2 * expert])
        second_half = expert_half(block_rows, w_gate[2 * expert + 1], w_up[2 * expert + 1], w_down[2 * expert + 1])
        return first_half.astype(jnp.float32) + second_half.astype(jnp.float32)
    summed = lax.map(run_expert, jnp.arange(experts, dtype=jnp.int32)).reshape(experts * slot_total, D)
    mixed_out = (gates_row.reshape(-1)[:, None] * summed[places]).reshape(FRAMES, 2, D).sum(1)
    resid = hidden_row + mixed_out
    return jnp.dot((rms_scale(resid) * final_gain).astype(jnp.bfloat16), w_out, preferred_element_type=jnp.float32)

def attend(advanced, modulation_row, w_in, w_qkv):
    embedded = jnp.dot(advanced.astype(jnp.bfloat16), w_in, preferred_element_type=jnp.float32)
    modulated = (rms_scale(embedded) * modulation_row[1] + modulation_row[0]).astype(jnp.bfloat16)
    projected = jnp.dot(modulated, w_qkv, preferred_element_type=jnp.float32).astype(jnp.bfloat16)
    head_width = HEADS * HDIM
    queries = projected[:, :head_width].reshape(FRAMES, HEADS, HDIM).astype(jnp.float32)
    key_cols = projected[:, head_width:2 * head_width].reshape(FRAMES, HEADS, HDIM).astype(jnp.float32)
    value_cols = projected[:, 2 * head_width:].reshape(FRAMES, HEADS, HDIM).astype(jnp.float32)
    score_scale = 1.0 / math.sqrt(HDIM)
    scores = jnp.einsum('thd,nhd->htn', queries, key_cols, precision=lax.Precision.HIGHEST) * score_scale
    weights = jax.nn.softmax(scores, -1)
    output = jnp.einsum('htn,nhd->thd', weights, value_cols, precision=lax.Precision.HIGHEST)
    return output.reshape(FRAMES, head_width).astype(jnp.bfloat16)

def reference(hidden, moe_gain, expert_ids, gate_weights, w_gate, w_up, w_down, final_gain, w_out, latent, w_in, modulation, w_qkv):
    velocities = [group_velocity(hidden[member], expert_ids[member], gate_weights[member], moe_gain, w_gate, w_up, w_down, final_gain, w_out) for member in range(N_PAIR)]
    next_rows = []
    attended_rows = []
    for member in range(N_PAIR):
        leader = member - member % 2
        cond_vel = velocities[leader]
        uncond_vel = velocities[leader + 1]
        guided = uncond_vel + GUIDANCE * (cond_vel - uncond_vel)
        advanced = jnp.concatenate([latent[leader], latent[leader + 1]], -1) + STEP_SIZE * guided
        half_index = member % 2
        next_rows.append(advanced[:, half_index * CH:(half_index + 1) * CH])
        attended_rows.append(attend(advanced, modulation[member], w_in, w_qkv))
    return (jnp.stack(next_rows), jnp.stack(attended_rows))
```

```python
import math

import jax
import jax.numpy as jnp
from jax import lax
from jax.experimental import pallas as pl
from jax.experimental.pallas import tpu as pltpu
from jax.sharding import Mesh
from jax.sharding import PartitionSpec as P

HDIM = 128
EPSILON = 1e-06
GUIDANCE = 3.0
STEP_SIZE = 0.25
CAP = 4
EP = ("x", "z", "core")
F32 = jnp.float32
BF16 = jnp.bfloat16
VMEM_LIMIT = 60 * 1024 * 1024


def vmem():
    return pl.BlockSpec(memory_space=pltpu.VMEM)


def slot_pick(ids_t, rows, frames):
    row = lax.broadcasted_iota(jnp.int32, (rows, frames), 0)
    expert = row >> 3
    slot = (row & (CAP - 1)).astype(F32)
    first = ids_t[0:1, :] == expert
    second = ids_t[1:2, :] == expert
    member = jnp.where(first | second, 1.0, 0.0)
    earlier = lax.broadcasted_iota(jnp.int32, (frames, frames), 0) < lax.broadcasted_iota(
        jnp.int32, (frames, frames), 1
    )
    rank = jnp.dot(
        member.astype(BF16), jnp.where(earlier, 1.0, 0.0).astype(BF16), preferred_element_type=F32
    )
    taken = (member > 0.0) & (rank == slot)
    return taken, first


def front_kernel(hidden_ref, gain_ref, ids_ref, out_ref):
    hidden = hidden_ref[...]
    frames, width = hidden.shape
    half = width // 2
    rows = out_ref.shape[0]
    mean = jnp.mean(hidden * hidden, -1, keepdims=True)
    normed = (hidden * lax.rsqrt(mean + EPSILON) * gain_ref[...]).astype(BF16)
    taken, _ = slot_pick(ids_ref[...], rows, frames)
    pick = jnp.where(taken, 1.0, 0.0).astype(BF16)
    low = jnp.dot(pick, normed[:, :half], preferred_element_type=F32)
    high = jnp.dot(pick, normed[:, half:], preferred_element_type=F32)
    row = lax.broadcasted_iota(jnp.int32, (rows, 1), 0)
    out_ref[...] = jnp.where((row & CAP) == 0, low, high).astype(BF16)


def expert_kernel(rows_ref, gate_ref, up_ref, down_ref, out_ref):
    rows = rows_ref[...]
    gated = jnp.dot(rows, gate_ref[...], preferred_element_type=F32)
    upward = jnp.dot(rows, up_ref[...], preferred_element_type=F32)
    active = (gated * jax.nn.sigmoid(gated) * upward).astype(BF16)
    out_ref[...] = jnp.dot(active, down_ref[...], preferred_element_type=F32).astype(BF16)


def experts(all_rows, gate_mat, up_mat, down_mat, block):
    total, width = all_rows.shape
    quarter = gate_mat.shape[1]
    return pl.pallas_call(
        expert_kernel,
        grid=(total // block,),
        in_specs=[
            pl.BlockSpec((block, width), lambda i: (i, 0)),
            pl.BlockSpec((width, quarter), lambda i: (0, 0)),
            pl.BlockSpec((width, quarter), lambda i: (0, 0)),
            pl.BlockSpec((quarter, width), lambda i: (0, 0)),
        ],
        out_specs=pl.BlockSpec((block, width), lambda i: (i, 0)),
        out_shape=jax.ShapeDtypeStruct((total, width), BF16),
        compiler_params=pltpu.CompilerParams(vmem_limit_bytes=VMEM_LIMIT),
        name="experts",
    )(all_rows, gate_mat, up_mat, down_mat)


def combine_kernel(back_ref, ids_ref, gates_ref, hidden_ref, gain_ref, w_out_ref, out_ref):
    hidden = hidden_ref[...]
    frames, width = hidden.shape
    half = width // 2
    rows = back_ref.shape[0]
    taken, first = slot_pick(ids_ref[...], rows, frames)
    weight = jnp.where(first, gates_ref[0:1, :], gates_ref[1:2, :])
    weight = jnp.where(taken, weight, 0.0)
    row = lax.broadcasted_iota(jnp.int32, (rows, frames), 0)
    back = back_ref[...]

    def gather(mat):
        top = mat.astype(BF16)
        rest = mat - top.astype(F32)
        mid = rest.astype(BF16)
        last = (rest - mid.astype(F32)).astype(BF16)
        dims = (((0,), (0,)), ((), ()))
        total = lax.dot_general(last, back, dims, preferred_element_type=F32)
        total = total + lax.dot_general(mid, back, dims, preferred_element_type=F32)
        return total + lax.dot_general(top, back, dims, preferred_element_type=F32)

    low = gather(jnp.where((row & CAP) == 0, weight, 0.0))
    high = gather(jnp.where((row & CAP) == 0, 0.0, weight))
    resid = hidden + jnp.concatenate([low, high], 1)
    mean = jnp.mean(resid * resid, -1, keepdims=True)
    scaled = (resid * lax.rsqrt(mean + EPSILON) * gain_ref[...]).astype(BF16)
    out_ref[...] = jnp.dot(scaled, w_out_ref[...], preferred_element_type=F32)


def attend_kernel(
    where_ref, adv_ref, w_in_ref, mod_ref, w_head_ref, out_ref, key_ref, value_ref, query_ref
):
    frames = adv_ref.shape[0]
    tok = 32
    block = 256
    w_in = w_in_ref[...]
    shift = mod_ref[0:1, :]
    scale = mod_ref[1:2, :]

    def modulate(adv):
        embedded = jnp.dot(adv, w_in, preferred_element_type=F32)
        mean = jnp.mean(embedded * embedded, -1, keepdims=True)
        return (embedded * lax.rsqrt(mean + EPSILON) * scale + shift).astype(BF16)

    pos = where_ref[0]
    for part in range(8):
        start = pl.multiple_of((part // 2) * 512 + pos * 64 + (part % 2) * tok, tok)
        query_ref[part * tok : (part + 1) * tok, :] = adv_ref[pl.ds(start, tok), :]
    query = jnp.dot(
        modulate(query_ref[...]), w_head_ref[where_ref[1]], preferred_element_type=F32
    ).astype(BF16)
    w_key = w_head_ref[where_ref[2]]
    w_value = w_head_ref[where_ref[3]]
    for i in range(frames // block):
        rows = modulate(adv_ref[i * block : (i + 1) * block, :])
        key_ref[i * block : (i + 1) * block, :] = jnp.dot(
            rows, w_key, preferred_element_type=F32
        ).astype(BF16)
        value_ref[i * block : (i + 1) * block, :] = jnp.dot(
            rows, w_value, preferred_element_type=F32
        ).astype(BF16)
    scores = lax.dot_general(
        query, key_ref[...], (((1,), (1,)), ((), ())), preferred_element_type=F32
    ) * (1.0 / math.sqrt(HDIM))
    weights = jnp.exp(scores - jnp.max(scores, 1, keepdims=True))
    total = jnp.sum(weights, 1, keepdims=True)
    mixed = jnp.dot(weights.astype(BF16), value_ref[...], preferred_element_type=F32)
    out_ref[...] = (mixed / total).astype(BF16)


def per_device(
    hidden,
    moe_gain,
    expert_ids,
    gate_weights,
    w_gate,
    w_up,
    w_down,
    final_gain,
    w_out,
    latent,
    w_in,
    modulation,
    w_qkv,
):
    tok_rows, width = hidden.shape[1:]
    n_chip = lax.axis_size("x") * lax.axis_size("z")
    n_pair = lax.axis_size("pair")
    own_hidden = hidden[0]
    ids_t = expert_ids[0].T
    gates_t = gate_weights[0].T
    gain_row = moe_gain.reshape(1, width)
    pair = lax.axis_index("pair")
    swap = [(i, i ^ 1) for i in range(n_pair)]

    head = lax.axis_index("x") * 2 + lax.axis_index("core")
    per_pair = w_qkv.shape[1] // HDIM
    n_head = n_pair * per_pair // 3
    ahead = (per_pair * pair - head + n_head - 1) // n_head
    local = jnp.clip(head + n_head * ahead - per_pair * pair, 0, per_pair - 1)
    w_mine = lax.dynamic_slice(w_qkv, (0, local * HDIM), (width, HDIM))
    w_head = lax.all_gather(w_mine, "pair", axis=0, tiled=False)
    where = jnp.stack(
        [
            lax.axis_index("z"),
            head // per_pair,
            (head + n_head) // per_pair,
            (head + 2 * n_head) // per_pair,
        ]
    ).astype(jnp.int32)

    rows = 2 * CAP * n_chip
    buffers = pl.pallas_call(
        front_kernel,
        in_specs=[vmem(), vmem(), vmem()],
        out_specs=vmem(),
        out_shape=jax.ShapeDtypeStruct((rows, width // 2), BF16),
        name="front",
    )(own_hidden, gain_row, ids_t)
    arrived = lax.all_to_all(buffers, ("x", "z"), split_axis=0, concat_axis=0, tiled=True)
    slots = n_chip * CAP
    out_row = lax.broadcasted_iota(jnp.int32, (slots, rows), 0)
    in_row = lax.broadcasted_iota(jnp.int32, (slots, rows), 1)
    low_at = (out_row // CAP) * 2 * CAP + out_row % CAP
    low_pick = (in_row == low_at).astype(BF16)
    high_pick = (in_row == low_at + CAP).astype(BF16)
    own_rows = jnp.concatenate(
        [
            jnp.dot(low_pick, arrived, preferred_element_type=F32).astype(BF16),
            jnp.dot(high_pick, arrived, preferred_element_type=F32).astype(BF16),
        ],
        1,
    )
    all_rows = lax.all_gather(own_rows, ("pair", "core"), axis=0, tiled=True)
    partial = experts(all_rows, w_gate[0], w_up[0], w_down[0], 256)
    summed = lax.psum_scatter(partial, ("pair", "core"), scatter_dimension=0, tiled=True)
    split = jnp.dot(low_pick.T, summed[:, : width // 2], preferred_element_type=F32) + jnp.dot(
        high_pick.T, summed[:, width // 2 :], preferred_element_type=F32
    )
    back = lax.all_to_all(
        split.astype(BF16), ("x", "z"), split_axis=0, concat_axis=0, tiled=True
    )
    velocity = pl.pallas_call(
        combine_kernel,
        in_specs=[vmem()] * 6,
        out_specs=vmem(),
        out_shape=jax.ShapeDtypeStruct((tok_rows, w_out.shape[1]), F32),
        name="combine",
    )(back, ids_t, gates_t, own_hidden, final_gain.reshape(1, width), w_out)

    own_latent = latent[0]
    partner_latent = lax.ppermute(own_latent, "pair", swap)
    partner_vel = lax.ppermute(velocity, "pair", swap)
    is_cond = pair % 2 == 0
    cond_vel = jnp.where(is_cond, velocity, partner_vel)
    uncond_vel = jnp.where(is_cond, partner_vel, velocity)
    guided = uncond_vel + GUIDANCE * (cond_vel - uncond_vel)
    whole_latent = jnp.where(
        is_cond,
        jnp.concatenate([own_latent, partner_latent], 1),
        jnp.concatenate([partner_latent, own_latent], 1),
    )
    advanced = whole_latent + STEP_SIZE * guided
    half_width = own_latent.shape[1]
    own_next = jnp.where(is_cond, advanced[:, :half_width], advanced[:, half_width:])

    copies = jnp.broadcast_to(
        advanced.astype(BF16)[None], (lax.axis_size(EP),) + advanced.shape
    ).reshape(-1, advanced.shape[1])
    all_adv = lax.all_to_all(copies, EP, split_axis=0, concat_axis=0, tiled=True)
    frames = all_adv.shape[0]
    queries = n_head * tok_rows
    mixed = pl.pallas_call(
        attend_kernel,
        in_specs=[pl.BlockSpec(memory_space=pltpu.SMEM)] + [vmem()] * 4,
        out_specs=vmem(),
        out_shape=jax.ShapeDtypeStruct((queries, HDIM), BF16),
        scratch_shapes=[
            pltpu.VMEM((frames, HDIM), BF16),
            pltpu.VMEM((frames, HDIM), BF16),
            pltpu.VMEM((queries, advanced.shape[1]), BF16),
        ],
        compiler_params=pltpu.CompilerParams(vmem_limit_bytes=VMEM_LIMIT),
        name="attend",
    )(where, all_adv, w_in, modulation[0], w_head)
    heads = lax.all_to_all(mixed, ("x", "core"), split_axis=0, concat_axis=0, tiled=True)
    attended = heads.reshape(n_head, tok_rows, HDIM).transpose(1, 0, 2).reshape(tok_rows, -1)
    return (own_next[None], attended[None])


def solution(mesh):
    chips = Mesh(mesh.devices.reshape(4, 4, 8, 2), ("pair", "x", "z", "core"))
    return jax.shard_map(
        per_device,
        mesh=chips,
        in_specs=(
            P("pair", EP, None),
            P(),
            P("pair", EP, None),
            P("pair", EP, None),
            P(EP, None, "pair"),
            P(EP, None, "pair"),
            P(EP, "pair", None),
            P(),
            P(),
            P("pair", EP, None),
            P(),
            P("pair", None, None),
            P(None, "pair"),
        ),
        out_specs=(P("pair", EP, None), P("pair", EP, None)),
        check_vma=False,
    )
```
